32 devices in a mesh: section: 2 (over core), ctx: 4 (over z), mp: 4 (over y, x).
Axes of the slice: x: 2, y: 2, z: 4, core: 2. Of those that a mesh axis runs over, the one named last changes fastest.
Arguments:
- frames: bfloat16 [2, 16, 128, 512], P('section', 'ctx'), may hold values from -6 to 6
- w_conv: bfloat16 [3, 512, 512], replicated, may hold values from -0.15625 to 0.15625
- w_lat: bfloat16 [512, 16], replicated, may hold values from -0.25 to 0.25
- dest: int32 [2, 512, 1], P(None, 'ctx'), may hold values from 0 to 3; in each aligned block of 128 rows (0 to 127, 128 to 255, ..., all dimensions but the last counted through in order) at most 48 rows name the same one
- pick: int32 [2, 512], P(None, 'ctx'), may hold values from 0 to 6
- w_embed: bfloat16 [64, 6144], replicated, may hold values from -0.75 to 0.75
- gain: float32 [6144], replicated, may hold values from 0.25 to 1.75
- w_qkv: bfloat16 [6144, 3, 4096], P(None, None, 'mp'), may hold values from -0.078125 to 0.078125
Outputs:
- attended: bfloat16 [2, 768, 4096], P('section', 'ctx', 'mp')
The draws below stay inside these ranges and needn't reach their ends.
Inputs may be any that keep to these rules, and one draw needn't show every extreme that they name: `dest`: among the 128 rows of one frame block, at most 48 name the same context shard, and some frame block reaches 48.
All inputs are finite; a program needn't handle non-finite values.
Results may differ from the reference program's by a relative error of at most 0.0061.
Values may be sent and summed in bfloat16 or wider, within the bound.
A program may use at most 128 MiB of HBM per device.

```python
import math
import jax
import jax.numpy as jnp
import numpy as np
from jax import lax

D = 6144
HEAD = 128
HEADS = 32
C_ENC = 512
LATC = 16
LATENT = 64
FRAMES = 4
CELLS = 128
GROUP = 4
ROWS = 128
NGROUP = 1
CAP = 48
TOKENS = 512
N_CTX = 4


def set_ends(values, own_key, least, high):
    longest = values.shape.index(max(values.shape))
    spots = []
    for shift in (0, 1):
        where = [jax.random.randint(jax.random.fold_in(own_key, axis), (), 0, length) for axis, length in enumerate(values.shape)]
        where[longest] = (where[longest] + shift) % values.shape[longest]
        spots.append(tuple(where))
    return values.at[spots[0]].set(least).at[spots[1]].set(high)


def level_of(stream_key, dims, pieces, smallest, top_value):
    level = 1.0
    for dim, parts in pieces:
        steps = jax.random.uniform(jax.random.fold_in(jax.random.fold_in(stream_key, 6), dim), (parts,), jnp.float32, smallest / len(pieces), top_value / len(pieces))
        level = level * jnp.repeat(jnp.exp(steps), dims[dim] // parts).reshape((-1,) + (1,) * (len(dims) - 1 - dim))
    return level


def assign_block(key, own, number, rows, number_of, top, limit, skew):
    order = jax.random.permutation(key, number_of)
    packed, ordinary = shares(number_of, rows * top, limit, skew, True), shares(number_of, rows * top, limit, skew, False)
    places = jnp.arange(number_of)

    def named(tallies, offset_by):
        used = int((tallies > 0).sum())
        fixed = max(1, used // 4)
        moved = fixed + (places - fixed + offset_by * (used - fixed)) % max(1, number_of - fixed)
        return jnp.zeros((number_of,), jnp.int32).at[order[jnp.where(places < fixed, places, moved)]].set(jnp.asarray(tallies, jnp.int32))

    tallies = jnp.where(number % 4 == 0, named(packed, number // 4), named(ordinary, number - number // 4 - 1))
    mixed = jax.random.permutation(jax.random.fold_in(own, 3), number_of)
    donor, sink = mixed[0:number_of // 2 * 2:2], mixed[1:number_of // 2 * 2:2]
    room = jnp.minimum(tallies[donor] - 1, limit - tallies[sink]) // 2
    room = jnp.where((donor == order[0]) | (sink == order[0]) | (tallies[sink] == 0), 0, jnp.maximum(room, 0))
    moved = jax.random.randint(jax.random.fold_in(own, 4), (number_of // 2,), 0, 1 << 20) % (room + 1)
    tallies = tallies.at[donor].add(-moved).at[sink].add(moved)
    members = jnp.searchsorted(jnp.cumsum(tallies), jnp.arange(rows * top), side="right").astype(jnp.int32)
    grid = members.reshape(top, rows).T
    grid = grid[jax.random.permutation(jax.random.fold_in(own, 1), rows)]
    offset_by = jax.random.randint(jax.random.fold_in(own, 2), (rows, 1), 0, top)
    return jnp.take_along_axis(grid, (jnp.arange(top)[None, :] + offset_by) % top, axis=1)


def shares(count, total, most, slope, full):
    loads = [(1 << 20) // math.isqrt(standing ** slope) + 1 for standing in range(1, count + 1)]
    largest = most if full else min(most, max(-(-total // count), total * loads[0] // sum(loads)))
    least = 1 if total - largest >= count - 1 else 0
    counts, spare = [largest] + [least] * (count - 1), total - largest - least * (count - 1)
    while spare > 0:
        movable = [i for i in range(1, count) if counts[i] < largest] or [i for i in range(1, count) if counts[i] < most]
        whole, budget = sum([loads[i] for i in movable]), spare
        for i in movable:
            extra = min(most - counts[i], max(1, budget * loads[i] // whole), spare)
            counts[i] = counts[i] + extra
            spare = spare - extra
    return np.array(counts)


def gaussian(rng, extent, spread, bound, pieces=(), held_as=jnp.bfloat16):
    array = spread * jax.random.normal(rng, extent, jnp.float32)
    if pieces:
        array = array * level_of(rng, extent, pieces, -0.22, 0.18)
    return jnp.clip(array, -bound, bound).astype(held_as)


def setup_inputs(seed: int = 0) -> dict:
    splits = jax.random.split(jax.random.key(seed), 9)
    frames = gaussian(splits[0], (2, N_CTX * FRAMES, CELLS, C_ENC), 1.0, 6.0, ((0, 2), (1, 4)))
    w_conv = gaussian(splits[1], (3, C_ENC, C_ENC), (3 * C_ENC) ** -0.5, 0.15625)
    w_lat = gaussian(splits[2], (C_ENC, LATC), C_ENC ** -0.5, 0.25)
    dest_keys = jax.random.split(jax.random.fold_in(splits[3], 1), 2 * TOKENS // ROWS)
    dest_turns = jax.random.permutation(jax.random.fold_in(splits[3], 3), 2 * TOKENS // ROWS)
    dest = jax.vmap(lambda own, number: assign_block(jax.random.fold_in(splits[3], 2), own, number, ROWS, N_CTX, 1, CAP, 2))(dest_keys, dest_turns).reshape((2, TOKENS, 1))
    pick = set_ends(jax.random.randint(splits[4], (2, TOKENS), 0, 7), jax.random.fold_in(splits[4], 1), 0, 6).astype(jnp.int32)
    w_embed = gaussian(splits[5], (LATENT, D), LATENT ** -0.5, 0.75)
    gain = jnp.clip(1.0 + 0.15 * jax.random.normal(splits[6], (D,), jnp.float32), 0.25, 1.75)
    w_qkv = gaussian(splits[7], (D, 3, HEADS * HEAD), D ** -0.5, 0.078125, ((2, 4),))
    return {"frames": frames, "w_conv": w_conv, "w_lat": w_lat, "dest": dest, "pick": pick, "w_embed": w_embed, "gain": gain, "w_qkv": w_qkv}


def encode(frame_block, w_conv, w_lat):
    frame_count = frame_block.shape[0]
    cells_here = frame_block.shape[1]
    channels = frame_block.shape[2]
    empty_frame = jnp.zeros_like(frame_block[:1])
    back_one = jnp.concatenate([empty_frame, frame_block[:-1]], axis=0)
    back_two = jnp.concatenate([empty_frame, empty_frame, frame_block[:-2]], axis=0)
    hidden = jnp.dot(frame_block.reshape(-1, channels), w_conv[0], preferred_element_type=jnp.float32)
    hidden = hidden + jnp.dot(back_one.reshape(-1, channels), w_conv[1], preferred_element_type=jnp.float32)
    hidden = hidden + jnp.dot(back_two.reshape(-1, channels), w_conv[2], preferred_element_type=jnp.float32)
    active = jax.nn.silu(hidden).astype(jnp.bfloat16)
    latent = jnp.dot(active, w_lat, preferred_element_type=jnp.float32).astype(jnp.bfloat16)
    return latent.reshape(frame_count, cells_here // 4, 4 * w_lat.shape[1])

def head_norm(values):
    return values * lax.rsqrt(lax.optimization_barrier(jnp.mean(values * values, axis=-1, keepdims=True)) + 1e-06)

def reference(frames, w_conv, w_lat, dest, pick, w_embed, gain, w_qkv):
    footage = frames.reshape(2, N_CTX, FRAMES, CELLS, C_ENC)
    results = []
    for section_slot in range(2):
        source = 1 - section_slot
        patch_rows = jnp.stack([encode(footage[source, shard], w_conv, w_lat).reshape(ROWS, LATENT) for shard in range(N_CTX)])
        targets = dest[source, :, 0].reshape(N_CTX, ROWS).astype(jnp.int32)
        choose = pick[source].reshape(N_CTX, ROWS).astype(jnp.int32)
        tier = (choose >= 4).astype(jnp.int32) + (choose >= 6).astype(jnp.int32)
        labels = targets // GROUP + NGROUP * tier + 1
        onehot = (targets[:, :, None] == jnp.arange(N_CTX, dtype=jnp.int32)[None, None, :]).astype(jnp.int32)
        before = jnp.cumsum(onehot, axis=1, dtype=jnp.int32) - onehot
        within = lax.optimization_barrier(jnp.sum(before * onehot, axis=2, dtype=jnp.int32))
        position = targets * (N_CTX * CAP) + jnp.arange(N_CTX, dtype=jnp.int32)[:, None] * CAP + within
        tokens = patch_rows.reshape(-1, LATENT)
        flat_labels = labels.reshape(-1)
        embedded = jnp.dot(tokens, w_embed, preferred_element_type=jnp.float32)
        normed = (embedded * lax.rsqrt(lax.optimization_barrier(jnp.mean(embedded * embedded, axis=-1, keepdims=True)) + 1e-06) * gain).astype(jnp.bfloat16)
        projected = jnp.dot(normed, w_qkv.reshape(D, -1), preferred_element_type=jnp.float32)
        projected = projected.reshape(-1, 3, HEADS, HEAD)
        queries = head_norm(projected[:, 0]).astype(jnp.bfloat16)
        keys_all = head_norm(projected[:, 1]).astype(jnp.bfloat16)
        values_all = projected[:, 2].astype(jnp.bfloat16)
        allowed = flat_labels[:, None] == flat_labels[None, :]
        factor = 1.0 / HEAD ** 0.5

        def one_head(operands):
            query_head, key_head, value_head = operands
            scores = jnp.dot(query_head, key_head.T, preferred_element_type=jnp.float32) * factor
            expo = jnp.where(allowed, jnp.exp(scores), 0.0)
            total = lax.optimization_barrier(jnp.sum(expo, axis=-1))
            summed = jnp.dot(expo.astype(jnp.bfloat16), value_head, preferred_element_type=jnp.float32)
            return summed / total[:, None]
        heads_out = lax.map(one_head, (queries.transpose(1, 0, 2), keys_all.transpose(1, 0, 2), values_all.transpose(1, 0, 2)))
        attended = heads_out.transpose(1, 0, 2).reshape(-1, HEADS * HEAD).astype(jnp.bfloat16)
        canvas = jnp.zeros((N_CTX * N_CTX * CAP, HEADS * HEAD), jnp.bfloat16)
        results.append(canvas.at[position.reshape(-1)].set(attended))
    return jnp.stack(results)
```

```python
import functools

import jax
import jax.numpy as jnp
from jax import lax
from jax.experimental import pallas as pl
from jax.experimental.pallas import tpu as pltpu
from jax.sharding import PartitionSpec as P

HEAD = 128
GROUP = 4
LANES = 128
META = 16
EPS = 1e-06
MESH = pl.DeviceIdType.MESH
F32 = jnp.float32
BF16 = jnp.bfloat16
HBM = pl.BlockSpec(memory_space=pltpu.HBM)
VMEM = pl.BlockSpec(memory_space=pltpu.VMEM)
LIMIT = 60 * 1024 * 1024


def dot(a, b):
    return jnp.dot(a, b, preferred_element_type=F32)


def dot_nt(a, b):
    return lax.dot_general(a, b, (((1,), (1,)), ((), ())), preferred_element_type=F32)


def iota(shape, dim):
    return lax.broadcasted_iota(jnp.int32, shape, dim)


def encode_kernel(
    shards, frame_count, pieces,
    frames_hbm, conv_hbm, lat_hbm, dest_hbm, pick_hbm, embed_hbm, gain_hbm, qkv_hbm,
    rows_out, meta_out, weff_out,
    frames, conv, lat_ref, dest_ref, pick_ref, embed, gain_ref, qkv, scaled, wide, packed, meta_ref, total,
    in_sem, qkv_sem, row_send, row_recv, meta_send, meta_recv, half_send, half_recv,
):
    section = lax.axis_index("section")
    ctx = lax.axis_index("ctx")
    other = 1 - section
    depth = embed.shape[1]
    latent = embed.shape[0]
    half = qkv.shape[2]
    step = depth // pieces
    row_count = dest_ref.shape[2]
    pack = LANES // latent
    lines = row_count // pack

    barrier = pltpu.get_barrier_semaphore()
    for d in range(shards):
        pl.semaphore_signal(
            barrier, inc=1,
            device_id={"section": other, "ctx": lax.rem(ctx + d, shards)}, device_id_type=MESH,
        )
    loads = [
        pltpu.make_async_copy(source, target, in_sem.at[i])
        for i, (source, target) in enumerate((
            (dest_hbm, dest_ref), (pick_hbm, pick_ref), (lat_hbm, lat_ref),
            (frames_hbm, frames), (conv_hbm, conv), (embed_hbm, embed), (gain_hbm, gain_ref),
        ))
    ]
    for load in loads:
        load.start()
    columns = pl.ds(pl.multiple_of(section * half, LANES), half)

    def stream(j, p):
        part = pl.ds(pl.multiple_of(p * step, step), step)
        return pltpu.make_async_copy(
            qkv_hbm.at[j, part, columns], qkv.at[j, part, :], qkv_sem.at[j * pieces + p]
        )

    for j in range(3):
        for p in range(pieces):
            stream(j, p).start()

    def target(d):
        return {"section": other, "ctx": lax.rem(ctx + d, shards)}

    order = sorted(range(shards), key=lambda d: -min(d, shards - d))

    loads[0].wait()
    loads[1].wait()
    first = section == 0
    dest = jnp.where(first, dest_ref[0], dest_ref[1])
    pick = jnp.where(first, pick_ref[0:1, :], pick_ref[1:2, :])
    tier = (pick >= 4).astype(jnp.int32) + (pick >= 6).astype(jnp.int32)
    label = dest // GROUP + shards // GROUP * tier + 1
    padded = -(-shards // 8) * 8
    onehot = (iota((padded, row_count), 0) == dest).astype(F32)
    earlier = (iota((row_count, row_count), 0) < iota((row_count, row_count), 1)).astype(F32)
    before = dot(onehot.astype(BF16), earlier.astype(BF16))
    within = jnp.sum(before * onehot, axis=0, keepdims=True)
    line = iota((META, row_count), 0)
    meta = jnp.where(line == 0, dest.astype(F32), 0.0)
    meta = jnp.where(line == 1, within, meta)
    meta = jnp.where(line == 2, label.astype(F32), meta)
    meta_ref[...] = meta.astype(BF16)
    pl.semaphore_wait(barrier, shards)
    sends = []
    for d in order:
        send = pltpu.make_async_remote_copy(
            src_ref=meta_ref, dst_ref=meta_out.at[ctx],
            send_sem=meta_send.at[d], recv_sem=meta_recv.at[d],
            device_id=target(d), device_id_type=MESH,
        )
        send.start()
        sends.append(send)

    cells, channels = frames.shape
    frame = cells // frame_count
    classes = lat_ref.shape[0]
    per = latent // classes
    for load in loads[2:5]:
        load.wait()
    x = frames[...]
    back = [x]
    for t in range(1, conv.shape[0]):
        back.append(jnp.concatenate(
            [jnp.zeros((t * frame, channels), BF16), frames[: cells - t * frame, :]], axis=0
        ))
    x = jnp.concatenate(back, axis=1)
    narrow = lat_ref[...]
    spread = jnp.concatenate([narrow] * (LANES // classes), axis=0)
    chunk = 256
    for n in range(channels // chunk):
        part = slice(n * chunk, (n + 1) * chunk)
        taps = jnp.concatenate([conv[t, :, part] for t in range(conv.shape[0])], axis=0)
        value = dot(x, taps)
        active = (value * jax.nn.sigmoid(value)).astype(BF16)
        partial = dot_nt(active, spread[:, part])
        if n == 0:
            wide[...] = partial
        else:
            wide[...] += partial
    for load in loads[5:]:
        load.wait()
    gram = dot_nt(embed[...], embed[...]) * (1.0 / depth)
    patches = jnp.zeros((row_count, LANES), F32)
    lane = iota((row_count, LANES), 1)
    for i in range(per):
        cell = wide[pl.ds(i, row_count, stride=per), :].astype(BF16).astype(F32)
        patches = jnp.where(lane // classes == i, cell, patches)
    slim = patches[:, :latent]
    exact = slim.astype(BF16)
    image = jnp.zeros((row_count, latent), F32)
    rest = gram
    for _ in range(3):
        piece = rest.astype(BF16)
        rest = rest - piece.astype(F32)
        image = image + dot(exact, piece)
    square = jnp.sum(slim * image, axis=1, keepdims=True)
    patches = patches * lax.rsqrt(jnp.maximum(square, 0.0) + EPS)
    joined = patches[:lines, :]
    for i in range(1, pack):
        joined = joined + pltpu.roll(patches[i * lines : (i + 1) * lines, :], i * latent, 1)
    packed[...] = joined.astype(BF16)

    for d in order:
        send = pltpu.make_async_remote_copy(
            src_ref=packed, dst_ref=rows_out.at[ctx],
            send_sem=row_send.at[d], recv_sem=row_recv.at[d],
            device_id=target(d), device_id_type=MESH,
        )
        send.start()
        sends.append(send)

    tile = 512
    for k in range(depth // tile):
        part = slice(k * tile, (k + 1) * tile)
        full = embed[:, part].astype(F32) * gain_ref[:, part]
        top = full.astype(BF16)
        scaled[:latent, part] = top
        scaled[latent:, part] = (full - top.astype(F32)).astype(BF16)

    def swap(j):
        return pltpu.make_async_remote_copy(
            src_ref=weff_out.at[section, j], dst_ref=weff_out.at[section, j],
            send_sem=half_send.at[j], recv_sem=half_recv.at[j],
            device_id={"section": other}, device_id_type=MESH,
        )

    def contract(j, carry):
        total[...] = jnp.zeros_like(total)

        def piece(p, inner):
            stream(j, p).wait()
            part = pl.ds(pl.multiple_of(p * step, step), step)
            total[...] += dot(scaled[:, part], qkv[j, part, :])
            return inner

        lax.fori_loop(0, pieces, piece, 0)
        full = total[...]
        weff_out[section, j] = (full[:latent] + full[latent:]).astype(BF16)
        swap(j).start()
        return carry

    lax.fori_loop(0, 3, contract, 0)
    for send in sends:
        send.wait()
    for j in range(3):
        swap(j).wait()


def attend_kernel(shards, capacity, rows_ref, meta_ref, weff_ref, out_hbm, out_ref, sem):
    ctx = lax.axis_index("ctx")
    sections, _, latent, half = weff_ref.shape
    lines = rows_ref.shape[1]
    pack = LANES // latent
    slots = out_ref.shape[0]
    blocks, labels, spots = [], [], []
    for source in range(shards):
        meta = meta_ref[source].astype(F32)
        labels.append(meta[2:3, :])
        home = meta[1:2, :] + (source * capacity)
        spots.append(jnp.where(meta[0:1, :] == ctx.astype(F32), home, -1.0))
        both = rows_ref[source]
        for i in range(pack):
            blocks.append(both[:, i * latent : (i + 1) * latent])
    rows = jnp.concatenate(blocks, axis=0)
    label = jnp.concatenate(labels, axis=1)
    spot = jnp.concatenate(spots, axis=1).astype(jnp.int32)
    taken = spot == iota((slots, spot.shape[1]), 0)
    picked = dot(taken.astype(F32).astype(BF16), rows).astype(BF16)
    own = jnp.sum(jnp.where(taken, label, 0.0), axis=1, keepdims=True)
    bias = jnp.where(label == own, 0.0, -1e30)

    def head_norm(x, factor):
        return x * (lax.rsqrt(jnp.mean(x * x, axis=-1, keepdims=True) + EPS) * factor)

    copies = []
    group = min(2, half // HEAD)
    pair = group * HEAD
    for i in range(sections):
        for g in range(half // pair):
            cols = slice(g * pair, (g + 1) * pair)
            q = dot(picked, weff_ref[i, 0, :, cols])
            k = dot(rows, weff_ref[i, 1, :, cols])
            v = dot(rows, weff_ref[i, 2, :, cols]).astype(BF16)
            for h in range(group):
                part = slice(h * HEAD, (h + 1) * HEAD)
                queries = head_norm(q[:, part], 1.0 / HEAD**0.5).astype(BF16)
                keys = head_norm(k[:, part], 1.0).astype(BF16)
                expo = jnp.exp(dot_nt(queries, keys) + bias)
                den = jnp.sum(expo, axis=1, keepdims=True)
                summed = dot(expo.astype(BF16), v[:, part])
                where = slice(i * half + g * pair + h * HEAD, i * half + g * pair + (h + 1) * HEAD)
                out_ref[:, where] = (summed * (1.0 / jnp.where(den > 0.0, den, 1.0))).astype(BF16)
            where = pl.ds(i * half + g * pair, pair)
            copy = pltpu.make_async_copy(out_ref.at[:, where], out_hbm.at[:, where], sem.at[len(copies)])
            copy.start()
            copies.append(copy)
    for copy in copies:
        copy.wait()


def on_device(shards, sections, frames, w_conv, w_lat, dest, pick, w_embed, gain, w_qkv):
    _, frame_count, frame, channels = frames.shape
    latent, depth = w_embed.shape
    cells = frame_count * frame
    row_count = dest.shape[1]
    columns = w_qkv.shape[2]
    half = columns // sections
    pieces = 4
    capacity = max(2, 3 * row_count // (2 * shards))
    slots = shards * capacity
    lines = row_count * latent // LANES
    rows, meta, weff = pl.pallas_call(
        functools.partial(encode_kernel, shards, frame_count, pieces),
        out_shape=(
            pltpu.VMEM((shards, lines, LANES), BF16),
            pltpu.VMEM((shards, META, row_count), BF16),
            pltpu.VMEM((sections, 3, latent, half), BF16),
        ),
        in_specs=[HBM] * 8,
        out_specs=(VMEM, VMEM, VMEM),
        scratch_shapes=[
            pltpu.VMEM((cells, channels), BF16),
            pltpu.VMEM(w_conv.shape, BF16),
            pltpu.VMEM((w_lat.shape[1], channels), BF16),
            pltpu.VMEM((sections, 1, row_count), jnp.int32),
            pltpu.VMEM((sections, row_count), jnp.int32),
            pltpu.VMEM((latent, depth), BF16),
            pltpu.VMEM((1, depth), F32),
            pltpu.VMEM((3, depth, half), BF16),
            pltpu.VMEM((2 * latent, depth), BF16),
            pltpu.VMEM((cells, LANES), F32),
            pltpu.VMEM((lines, LANES), BF16),
            pltpu.VMEM((META, row_count), BF16),
            pltpu.VMEM((2 * latent, half), F32),
            pltpu.SemaphoreType.DMA((7,)),
            pltpu.SemaphoreType.DMA((3 * pieces,)),
            pltpu.SemaphoreType.DMA((shards,)),
            pltpu.SemaphoreType.DMA((shards,)),
            pltpu.SemaphoreType.DMA((shards,)),
            pltpu.SemaphoreType.DMA((shards,)),
            pltpu.SemaphoreType.DMA((3,)),
            pltpu.SemaphoreType.DMA((3,)),
        ],
        compiler_params=pltpu.CompilerParams(
            collective_id=0, has_side_effects=True, vmem_limit_bytes=LIMIT
        ),
    )(
        frames.reshape(cells, channels),
        w_conv,
        w_lat.T,
        dest.transpose(0, 2, 1),
        pick,
        w_embed,
        gain.reshape(1, depth),
        w_qkv.transpose(1, 0, 2),
    )
    out = pl.pallas_call(
        functools.partial(attend_kernel, shards, capacity),
        out_shape=jax.ShapeDtypeStruct((slots, columns), BF16),
        in_specs=[VMEM, VMEM, VMEM],
        out_specs=HBM,
        scratch_shapes=[
            pltpu.VMEM((slots, columns), BF16),
            pltpu.SemaphoreType.DMA((columns // HEAD,)),
        ],
        compiler_params=pltpu.CompilerParams(vmem_limit_bytes=LIMIT // 2),
    )(rows, meta, weff)
    return out.reshape(1, slots, columns)


def solution(mesh):
    in_specs = (
        P("section", "ctx", None, None),
        P(),
        P(),
        P(None, "ctx", None),
        P(None, "ctx"),
        P(),
        P(),
        P(None, None, "mp"),
    )
    return jax.shard_map(
        functools.partial(on_device, mesh.shape["ctx"], mesh.shape["section"]),
        mesh=mesh,
        in_specs=in_specs,
        out_specs=P("section", "ctx", "mp"),
        check_vma=False,
    )
```

```python
import functools

import jax
import jax.numpy as jnp
from jax import lax
from jax.experimental import pallas as pl
from jax.experimental.pallas import tpu as pltpu
from jax.sharding import PartitionSpec as P

HEAD = 128
GROUP = 4
LANES = 128
META = 16
EPS = 1e-06
MESH = pl.DeviceIdType.MESH
F32 = jnp.float32
BF16 = jnp.bfloat16
HBM = pl.BlockSpec(memory_space=pltpu.HBM)
VMEM = pl.BlockSpec(memory_space=pltpu.VMEM)
LIMIT = 60 * 1024 * 1024


def dot(a, b):
    return jnp.dot(a, b, preferred_element_type=F32)


def dot_nt(a, b):
    return lax.dot_general(a, b, (((1,), (1,)), ((), ())), preferred_element_type=F32)


def iota(shape, dim):
    return lax.broadcasted_iota(jnp.int32, shape, dim)


def encode_kernel(
    shards, frame_count, pieces,
    frames_hbm, conv_hbm, lat_hbm, dest_hbm, pick_hbm, embed_hbm, gain_hbm, qkv_hbm,
    rows_out, meta_out, weff_out,
    frames, conv, lat_ref, dest_ref, pick_ref, embed, gain_ref, qkv, scaled, wide, packed, meta_ref, total,
    in_sem, qkv_sem, row_send, row_recv, meta_send, meta_recv, half_send, half_recv,
):
    section = lax.axis_index("section")
    ctx = lax.axis_index("ctx")
    other = 1 - section
    depth = embed.shape[1]
    latent = embed.shape[0]
    half = qkv.shape[2]
    step = depth // pieces
    row_count = dest_ref.shape[2]
    pack = LANES // latent
    lines = row_count // pack

    barrier = pltpu.get_barrier_semaphore()
    for d in range(shards):
        pl.semaphore_signal(
            barrier, inc=1,
            device_id={"section": other, "ctx": lax.rem(ctx + d, shards)}, device_id_type=MESH,
        )
    loads = [
        pltpu.make_async_copy(source, target, in_sem.at[i])
        for i, (source, target) in enumerate((
            (dest_hbm, dest_ref), (pick_hbm, pick_ref), (lat_hbm, lat_ref), (gain_hbm, gain_ref),
            (embed_hbm, embed), (frames_hbm, frames), (conv_hbm, conv),
        ))
    ]
    for load in loads:
        load.start()
    columns = pl.ds(pl.multiple_of(section * half, LANES), half)

    def stream(j, p):
        part = pl.ds(pl.multiple_of(p * step, step), step)
        return pltpu.make_async_copy(
            qkv_hbm.at[j, part, columns], qkv.at[j, part, :], qkv_sem.at[j * pieces + p]
        )

    def target(d):
        return {"section": other, "ctx": lax.rem(ctx + d, shards)}

    order = sorted(range(shards), key=lambda d: -min(d, shards - d))

    loads[0].wait()
    loads[1].wait()
    first = section == 0
    dest = jnp.where(first, dest_ref[0], dest_ref[1])
    pick = jnp.where(first, pick_ref[0:1, :], pick_ref[1:2, :])
    tier = (pick >= 4).astype(jnp.int32) + (pick >= 6).astype(jnp.int32)
    label = dest // GROUP + shards // GROUP * tier + 1
    padded = -(-shards // 8) * 8
    onehot = (iota((padded, row_count), 0) == dest).astype(F32)
    earlier = (iota((row_count, row_count), 0) < iota((row_count, row_count), 1)).astype(F32)
    before = dot(onehot.astype(BF16), earlier.astype(BF16))
    within = jnp.sum(before * onehot, axis=0, keepdims=True)
    line = iota((META, row_count), 0)
    meta = jnp.where(line == 0, dest.astype(F32), 0.0)
    meta = jnp.where(line == 1, within, meta)
    meta = jnp.where(line == 2, label.astype(F32), meta)
    meta_ref[...] = meta.astype(BF16)
    cells, channels = frames.shape
    frame = cells // frame_count
    classes = lat_ref.shape[0]
    per = latent // classes
    for load in loads[2:5]:
        load.wait()
    for j in range(1):
        for p in range(pieces):
            stream(j, p).start()

    tile = 512
    for k in range(depth // tile):
        part = slice(k * tile, (k + 1) * tile)
        full = embed[:, part].astype(F32) * gain_ref[:, part]
        top = full.astype(BF16)
        scaled[:latent, part] = top
        scaled[latent:, part] = (full - top.astype(F32)).astype(BF16)
    gram = dot_nt(embed[...], embed[...]) * (1.0 / depth)
    for load in loads[5:]:
        load.wait()
    for j in range(1, 3):
        for p in range(pieces):
            stream(j, p).start()

    x = frames[...]
    back = [x]
    for t in range(1, conv.shape[0]):
        back.append(jnp.concatenate(
            [jnp.zeros((t * frame, channels), BF16), frames[: cells - t * frame, :]], axis=0
        ))
    x = jnp.concatenate(back, axis=1)
    narrow = lat_ref[...]
    spread = jnp.concatenate([narrow] * (LANES // classes), axis=0)
    chunk = 256
    for n in range(channels // chunk):
        part = slice(n * chunk, (n + 1) * chunk)
        taps = jnp.concatenate([conv[t, :, part] for t in range(conv.shape[0])], axis=0)
        value = dot(x, taps)
        value = 0.5 * value
        active = (value * jnp.tanh(value) + value).astype(BF16)
        partial = dot_nt(active, spread[:, part])
        if n == 0:
            wide[...] = partial
        else:
            wide[...] += partial
    patches = jnp.zeros((row_count, LANES), F32)
    lane = iota((row_count, LANES), 1)
    for i in range(per):
        cell = wide[pl.ds(i, row_count, stride=per), :].astype(BF16).astype(F32)
        patches = jnp.where(lane // classes == i, cell, patches)
    slim = patches[:, :latent]
    exact = slim.astype(BF16)
    image = jnp.zeros((row_count, latent), F32)
    rest = gram
    for _ in range(3):
        piece = rest.astype(BF16)
        rest = rest - piece.astype(F32)
        image = image + dot(exact, piece)
    square = jnp.sum(slim * image, axis=1, keepdims=True)
    patches = patches * lax.rsqrt(jnp.maximum(square, 0.0) + EPS)
    joined = patches[:lines, :]
    for i in range(1, pack):
        joined = joined + pltpu.roll(patches[i * lines : (i + 1) * lines, :], i * latent, 1)
    packed[...] = joined.astype(BF16)

    def swap(j):
        return pltpu.make_async_remote_copy(
            src_ref=weff_out.at[section, j], dst_ref=weff_out.at[section, j],
            send_sem=half_send.at[j], recv_sem=half_recv.at[j],
            device_id={"section": other}, device_id_type=MESH,
        )

    def post(d):
        return pltpu.make_async_remote_copy(
            src_ref=packed, dst_ref=rows_out.at[ctx],
            send_sem=row_send.at[d], recv_sem=row_recv.at[d],
            device_id=target(d), device_id_type=MESH,
        )

    def post_meta(d):
        return pltpu.make_async_remote_copy(
            src_ref=meta_ref, dst_ref=meta_out.at[ctx],
            send_sem=meta_send.at[d], recv_sem=meta_recv.at[d],
            device_id=target(d), device_id_type=MESH,
        )

    def contract(j):
        total[...] = jnp.zeros_like(total)

        def piece(p, inner):
            stream(j, p).wait()
            part = pl.ds(pl.multiple_of(p * step, step), step)
            total[...] += dot(scaled[:, part], qkv[j, part, :])
            return inner

        lax.fori_loop(0, pieces, piece, 0)
        full = total[...]
        weff_out[section, j] = (full[:latent] + full[latent:]).astype(BF16)

    early = ctx == 0

    @pl.when(early)
    def _():
        contract(0)

    pl.semaphore_wait(barrier, shards)
    for d in order:
        post(d).start()
    for d in order:
        post_meta(d).start()

    @pl.when(jnp.logical_not(early))
    def _():
        contract(0)

    swap(0).start()

    def later(j, carry):
        contract(j)
        swap(j).start()
        return carry

    lax.fori_loop(1, 3, later, 0)
    for d in order:
        post(d).wait()
        post_meta(d).wait()
    for j in range(3):
        swap(j).wait()


def attend_kernel(shards, capacity, rows_ref, meta_ref, weff_ref, out_hbm, out_ref, sem):
    ctx = lax.axis_index("ctx")
    sections, _, latent, half = weff_ref.shape
    lines = rows_ref.shape[1]
    pack = LANES // latent
    slots = out_ref.shape[0]
    blocks, labels, spots = [], [], []
    for source in range(shards):
        meta = meta_ref[source].astype(F32)
        labels.append(meta[2:3, :])
        home = meta[1:2, :] + (source * capacity)
        spots.append(jnp.where(meta[0:1, :] == ctx.astype(F32), home, -1.0))
        both = rows_ref[source]
        for i in range(pack):
            blocks.append(both[:, i * latent : (i + 1) * latent])
    rows = jnp.concatenate(blocks, axis=0)
    label = jnp.concatenate(labels, axis=1)
    spot = jnp.concatenate(spots, axis=1).astype(jnp.int32)
    taken = spot == iota((slots, spot.shape[1]), 0)
    picked = dot(taken.astype(F32).astype(BF16), rows).astype(BF16)
    own = jnp.sum(jnp.where(taken, label, 0.0), axis=1, keepdims=True)
    bias = jnp.where(label == own, 0.0, -1e30)

    def head_norm(x, factor):
        return x * (lax.rsqrt(jnp.mean(x * x, axis=-1, keepdims=True) + EPS) * factor)

    copies = []
    group = min(2, half // HEAD)
    pair = group * HEAD
    for i in range(sections):
        for g in range(half // pair):
            cols = slice(g * pair, (g + 1) * pair)
            q = dot(picked, weff_ref[i, 0, :, cols])
            k = dot(rows, weff_ref[i, 1, :, cols])
            v = dot(rows, weff_ref[i, 2, :, cols]).astype(BF16)
            for h in range(group):
                part = slice(h * HEAD, (h + 1) * HEAD)
                queries = head_norm(q[:, part], 1.0 / HEAD**0.5).astype(BF16)
                keys = head_norm(k[:, part], 1.0).astype(BF16)
                expo = jnp.exp(dot_nt(queries, keys) + bias)
                den = jnp.sum(expo, axis=1, keepdims=True)
                summed = dot(expo.astype(BF16), v[:, part])
                where = slice(i * half + g * pair + h * HEAD, i * half + g * pair + (h + 1) * HEAD)
                out_ref[:, where] = (summed * (1.0 / jnp.where(den > 0.0, den, 1.0))).astype(BF16)
            where = pl.ds(i * half + g * pair, pair)
            copy = pltpu.make_async_copy(out_ref.at[:, where], out_hbm.at[:, where], sem.at[len(copies)])
            copy.start()
            copies.append(copy)
    for copy in copies:
        copy.wait()


def on_device(shards, sections, frames, w_conv, w_lat, dest, pick, w_embed, gain, w_qkv):
    _, frame_count, frame, channels = frames.shape
    latent, depth = w_embed.shape
    cells = frame_count * frame
    row_count = dest.shape[1]
    columns = w_qkv.shape[2]
    half = columns // sections
    pieces = 4
    capacity = max(2, 3 * row_count // (2 * shards))
    slots = shards * capacity
    lines = row_count * latent // LANES
    rows, meta, weff = pl.pallas_call(
        functools.partial(encode_kernel, shards, frame_count, pieces),
        out_shape=(
            pltpu.VMEM((shards, lines, LANES), BF16),
            pltpu.VMEM((shards, META, row_count), BF16),
            pltpu.VMEM((sections, 3, latent, half), BF16),
        ),
        in_specs=[HBM] * 8,
        out_specs=(VMEM, VMEM, VMEM),
        scratch_shapes=[
            pltpu.VMEM((cells, channels), BF16),
            pltpu.VMEM(w_conv.shape, BF16),
            pltpu.VMEM((w_lat.shape[1], channels), BF16),
            pltpu.VMEM((sections, 1, row_count), jnp.int32),
            pltpu.VMEM((sections, row_count), jnp.int32),
            pltpu.VMEM((latent, depth), BF16),
            pltpu.VMEM((1, depth), F32),
            pltpu.VMEM((3, depth, half), BF16),
            pltpu.VMEM((2 * latent, depth), BF16),
            pltpu.VMEM((cells, LANES), F32),
            pltpu.VMEM((lines, LANES), BF16),
            pltpu.VMEM((META, row_count), BF16),
            pltpu.VMEM((2 * latent, half), F32),
            pltpu.SemaphoreType.DMA((7,)),
            pltpu.SemaphoreType.DMA((3 * pieces,)),
            pltpu.SemaphoreType.DMA((shards,)),
            pltpu.SemaphoreType.DMA((shards,)),
            pltpu.SemaphoreType.DMA((shards,)),
            pltpu.SemaphoreType.DMA((shards,)),
            pltpu.SemaphoreType.DMA((3,)),
            pltpu.SemaphoreType.DMA((3,)),
        ],
        compiler_params=pltpu.CompilerParams(
            collective_id=0, has_side_effects=True, vmem_limit_bytes=LIMIT
        ),
    )(
        frames.reshape(cells, channels),
        w_conv,
        w_lat.T,
        dest.transpose(0, 2, 1),
        pick,
        w_embed,
        gain.reshape(1, depth),
        w_qkv.transpose(1, 0, 2),
    )
    out = pl.pallas_call(
        functools.partial(attend_kernel, shards, capacity),
        out_shape=jax.ShapeDtypeStruct((slots, columns), BF16),
        in_specs=[VMEM, VMEM, VMEM],
        out_specs=HBM,
        scratch_shapes=[
            pltpu.VMEM((slots, columns), BF16),
            pltpu.SemaphoreType.DMA((columns // HEAD,)),
        ],
        compiler_params=pltpu.CompilerParams(vmem_limit_bytes=LIMIT // 2),
    )(rows, meta, weff)
    return out.reshape(1, slots, columns)


def solution(mesh):
    in_specs = (
        P("section", "ctx", None, None),
        P(),
        P(),
        P(None, "ctx", None),
        P(None, "ctx"),
        P(),
        P(),
        P(None, None, "mp"),
    )
    return jax.shard_map(
        functools.partial(on_device, mesh.shape["ctx"], mesh.shape["section"]),
        mesh=mesh,
        in_specs=in_specs,
        out_specs=P("section", "ctx", "mp"),
        check_vma=False,
    )
```

```python
import functools

import jax
import jax.numpy as jnp
from jax import lax
from jax.experimental import pallas as pl
from jax.experimental.pallas import tpu as pltpu
from jax.sharding import PartitionSpec as P

HEAD = 128
GROUP = 4
LANES = 128
META = 16
EPS = 1e-06
MESH = pl.DeviceIdType.MESH
F32 = jnp.float32
BF16 = jnp.bfloat16
HBM = pl.BlockSpec(memory_space=pltpu.HBM)
VMEM = pl.BlockSpec(memory_space=pltpu.VMEM)
LIMIT = 40 * 1024 * 1024


def dot(a, b):
    return jnp.dot(a, b, preferred_element_type=F32)


def dot_nt(a, b):
    return lax.dot_general(a, b, (((1,), (1,)), ((), ())), preferred_element_type=F32)


def iota(shape, dim):
    return lax.broadcasted_iota(jnp.int32, shape, dim)


def encode_kernel(
    shards, frame_count, pieces,
    frames_hbm, conv_hbm, lat_hbm, dest_hbm, pick_hbm, embed_hbm, gain_hbm, qkv_hbm,
    weff_out, rows_out, queries_out, keys_out, bias_out,
    frames, conv, lat_ref, dest_ref, pick_ref, embed, gain_ref, qkv, scaled, wide, packed, inbox, total,
    in_sem, qkv_sem, row_send, row_recv, half_send, half_recv,
):
    section = lax.axis_index("section")
    ctx = lax.axis_index("ctx")
    other = 1 - section
    depth = embed.shape[1]
    latent = embed.shape[0]
    half = qkv.shape[2]
    step = depth // pieces
    row_count = dest_ref.shape[2]
    pack = LANES // latent
    lines = row_count // pack

    cells, channels = frames.shape
    chunks = 2
    chunk = channels // chunks

    barrier = pltpu.get_barrier_semaphore()
    for d in range(shards):
        pl.semaphore_signal(
            barrier, inc=1,
            device_id={"section": other, "ctx": lax.rem(ctx + d, shards)}, device_id_type=MESH,
        )
    loads = [
        pltpu.make_async_copy(source, target, in_sem.at[i])
        for i, (source, target) in enumerate((
            (dest_hbm, dest_ref), (pick_hbm, pick_ref), (lat_hbm, lat_ref), (gain_hbm, gain_ref),
            (embed_hbm, embed), (frames_hbm, frames),
        ) + tuple(
            (conv_hbm.at[:, :, pl.ds(n * chunk, chunk)], conv.at[:, :, pl.ds(n * chunk, chunk)])
            for n in range(chunks)
        ))
    ]
    for load in loads:
        load.start()
    columns = pl.ds(pl.multiple_of(section * half, LANES), half)

    def stream(j, p):
        part = pl.ds(pl.multiple_of(p * step, step), step)
        return pltpu.make_async_copy(
            qkv_hbm.at[j, part, columns], qkv.at[j, part, :], qkv_sem.at[j * pieces + p]
        )

    loads[0].wait()
    loads[1].wait()
    first = section == 0
    dest = jnp.where(first, dest_ref[0], dest_ref[1])
    pick = jnp.where(first, pick_ref[0:1, :], pick_ref[1:2, :])
    tier = (pick >= 4).astype(jnp.int32) + (pick >= 6).astype(jnp.int32)
    label = dest // GROUP + shards // GROUP * tier + 1
    padded = -(-shards // 8) * 8
    onehot = (iota((padded, row_count), 0) == dest).astype(F32)
    earlier = (iota((row_count, row_count), 0) < iota((row_count, row_count), 1)).astype(F32)
    before = dot(onehot.astype(BF16), earlier.astype(BF16))
    within = jnp.sum(before * onehot, axis=0, keepdims=True)
    line = iota((META, row_count), 0)
    meta = jnp.where(line == 0, dest.astype(F32), 0.0)
    meta = jnp.where(line == 1, within, meta)
    meta = jnp.where(line == 2, label.astype(F32), meta)
    packed[lines:, :] = meta.astype(BF16)
    frame = cells // frame_count
    classes = lat_ref.shape[0]
    per = latent // classes
    for load in loads[2:5]:
        load.wait()
    for j in range(1):
        for p in range(pieces):
            stream(j, p).start()

    tile = 512
    for k in range(depth // tile):
        part = slice(k * tile, (k + 1) * tile)
        full = embed[:, part].astype(F32) * gain_ref[:, part]
        top = full.astype(BF16)
        scaled[:latent, part] = top
        scaled[latent:, part] = (full - top.astype(F32)).astype(BF16)
    gram = dot_nt(embed[...], embed[...]) * (1.0 / depth)
    loads[5].wait()
    for j in range(1, 3):
        for p in range(pieces):
            stream(j, p).start()

    x = frames[...]
    back = [x]
    for t in range(1, conv.shape[0]):
        back.append(jnp.concatenate(
            [jnp.zeros((t * frame, channels), BF16), frames[: cells - t * frame, :]], axis=0
        ))
    x = jnp.concatenate(back, axis=1)
    narrow = lat_ref[...]
    spread = jnp.concatenate([narrow] * (LANES // classes), axis=0)
    for n in range(chunks):
        loads[6 + n].wait()
        part = slice(n * chunk, (n + 1) * chunk)
        taps = jnp.concatenate([conv[t, :, part] for t in range(conv.shape[0])], axis=0)
        value = dot(x, taps)
        value = 0.5 * value
        active = (value * jnp.tanh(value) + value).astype(BF16)
        partial = dot_nt(active, spread[:, part])
        if n == 0:
            wide[...] = partial
        else:
            wide[...] += partial
    patches = jnp.zeros((row_count, LANES), F32)
    lane = iota((row_count, LANES), 1)
    for i in range(per):
        cell = wide[pl.ds(i, row_count, stride=per), :].astype(BF16).astype(F32)
        patches = jnp.where(lane // classes == i, cell, patches)
    slim = patches[:, :latent]
    exact = slim.astype(BF16)
    image = jnp.zeros((row_count, latent), F32)
    rest = gram
    for _ in range(3):
        piece = rest.astype(BF16)
        rest = rest - piece.astype(F32)
        image = image + dot(exact, piece)
    square = jnp.sum(slim * image, axis=1, keepdims=True)
    patches = patches * lax.rsqrt(jnp.maximum(square, 0.0) + EPS)
    joined = patches[:lines, :]
    for i in range(1, pack):
        joined = joined + pltpu.roll(patches[i * lines : (i + 1) * lines, :], i * latent, 1)
    packed[:lines, :] = joined.astype(BF16)

    def swap(j):
        return pltpu.make_async_remote_copy(
            src_ref=weff_out.at[section, j], dst_ref=weff_out.at[section, j],
            send_sem=half_send.at[j], recv_sem=half_recv.at[j],
            device_id={"section": other}, device_id_type=MESH,
        )

    def post(t):
        return pltpu.make_async_remote_copy(
            src_ref=packed, dst_ref=inbox.at[ctx], send_sem=row_send.at[t], recv_sem=row_recv.at[ctx],
            device_id={"section": other, "ctx": t}, device_id_type=MESH,
        )

    def arrival(c):
        return pltpu.make_async_remote_copy(
            src_ref=packed, dst_ref=inbox.at[c], send_sem=row_send.at[c], recv_sem=row_recv.at[c],
            device_id={"section": other, "ctx": c}, device_id_type=MESH,
        )

    def contract(j):
        total[...] = jnp.zeros_like(total)

        def piece(p, inner):
            stream(j, p).wait()
            part = pl.ds(pl.multiple_of(p * step, step), step)
            total[...] += dot(scaled[:, part], qkv[j, part, :])
            return inner

        lax.fori_loop(0, pieces, piece, 0)
        full = total[...]
        weff_out[section, j] = (full[:latent] + full[latent:]).astype(BF16)

    early = ctx == 0

    @pl.when(early)
    def _():
        contract(0)

    pl.semaphore_wait(barrier, shards)
    for t in range(shards):
        post(t).start()

    @pl.when(jnp.logical_not(early))
    def _():
        contract(0)

    swap(0).start()

    def later(j, carry):
        contract(j)
        swap(j).start()
        return carry

    lax.fori_loop(1, 3, later, 0)
    sections = weff_out.shape[0]

    def head_norm(x, factor):
        return x * (lax.rsqrt(jnp.mean(x * x, axis=-1, keepdims=True) + EPS) * factor)

    def project(x, j, out, first_row, factor):
        count = x.shape[0]
        for i in range(sections):
            y = dot(x, weff_out[i, j])
            for h in range(half // HEAD):
                z = head_norm(y[:, h * HEAD : (h + 1) * HEAD], factor).astype(BF16)
                out[first_row : first_row + count, i * half + h * HEAD : i * half + (h + 1) * HEAD] = z

    swap(0).wait_recv()
    swap(1).wait_recv()
    capacity = queries_out.shape[0] // shards
    slots = queries_out.shape[0]
    labels, spots = [], []
    for c in range(shards):
        arrival(c).wait_recv()
        both = inbox[c, :lines, :]
        block = jnp.concatenate([both[:, i * latent : (i + 1) * latent] for i in range(pack)], axis=0)
        rows_out[c * row_count : (c + 1) * row_count, :] = block
        project(block, 1, keys_out, c * row_count, 1.0)
        meta = inbox[c, lines:, :].astype(F32)
        labels.append(meta[2:3, :])
        spots.append(jnp.where(meta[0:1, :] == ctx.astype(F32), meta[1:2, :] + (c * capacity), -1.0))
    label = jnp.concatenate(labels, axis=1)
    spot = jnp.concatenate(spots, axis=1).astype(jnp.int32)
    taken = spot == iota((slots, spot.shape[1]), 0)
    picked = dot(taken.astype(F32).astype(BF16), rows_out[...]).astype(BF16)
    own = jnp.sum(jnp.where(taken, label, 0.0), axis=1, keepdims=True)
    bias_out[...] = jnp.where(label == own, 0.0, -1e30)
    project(picked, 0, queries_out, 0, 1.0 / HEAD**0.5)
    for t in range(shards):
        post(t).wait_send()
    for j in range(3):
        swap(j).wait_send()
    swap(2).wait_recv()


def attend_kernel(weff_ref, rows_ref, queries_ref, keys_ref, bias_ref, out_hbm, out_ref, sem):
    sections, _, _, half = weff_ref.shape
    rows = rows_ref[...]
    copies = []
    group = min(2, half // HEAD)
    pair = group * HEAD
    for i in range(sections):
        for g in range(half // pair):
            v = dot(rows, weff_ref[i, 2, :, g * pair : (g + 1) * pair]).astype(BF16)
            for h in range(group):
                where = slice(i * half + g * pair + h * HEAD, i * half + g * pair + (h + 1) * HEAD)
                expo = jnp.exp(dot_nt(queries_ref[:, where], keys_ref[:, where]) + bias_ref[...])
                den = jnp.sum(expo, axis=1, keepdims=True)
                summed = dot(expo.astype(BF16), v[:, h * HEAD : (h + 1) * HEAD])
                out_ref[:, where] = (summed * (1.0 / jnp.where(den > 0.0, den, 1.0))).astype(BF16)
            where = pl.ds(i * half + g * pair, pair)
            copy = pltpu.make_async_copy(out_ref.at[:, where], out_hbm.at[:, where], sem.at[len(copies)])
            copy.start()
            copies.append(copy)
    for copy in copies:
        copy.wait()


def on_device(shards, sections, frames, w_conv, w_lat, dest, pick, w_embed, gain, w_qkv):
    _, frame_count, frame, channels = frames.shape
    latent, depth = w_embed.shape
    cells = frame_count * frame
    row_count = dest.shape[1]
    columns = w_qkv.shape[2]
    half = columns // sections
    pieces = 4
    capacity = max(2, 3 * row_count // (2 * shards))
    slots = shards * capacity
    lines = row_count * latent // LANES
    total_rows = shards * row_count
    handed = pl.pallas_call(
        functools.partial(encode_kernel, shards, frame_count, pieces),
        out_shape=(
            pltpu.VMEM((sections, 3, latent, half), BF16),
            pltpu.VMEM((total_rows, latent), BF16),
            pltpu.VMEM((slots, columns), BF16),
            pltpu.VMEM((total_rows, columns), BF16),
            pltpu.VMEM((slots, total_rows), F32),
        ),
        in_specs=[HBM] * 8,
        out_specs=(VMEM,) * 5,
        scratch_shapes=[
            pltpu.VMEM((cells, channels), BF16),
            pltpu.VMEM(w_conv.shape, BF16),
            pltpu.VMEM((w_lat.shape[1], channels), BF16),
            pltpu.VMEM((sections, 1, row_count), jnp.int32),
            pltpu.VMEM((sections, row_count), jnp.int32),
            pltpu.VMEM((latent, depth), BF16),
            pltpu.VMEM((1, depth), F32),
            pltpu.VMEM((3, depth, half), BF16),
            pltpu.VMEM((2 * latent, depth), BF16),
            pltpu.VMEM((cells, LANES), F32),
            pltpu.VMEM((lines + META, LANES), BF16),
            pltpu.VMEM((shards, lines + META, LANES), BF16),
            pltpu.VMEM((2 * latent, half), F32),
            pltpu.SemaphoreType.DMA((8,)),
            pltpu.SemaphoreType.DMA((3 * pieces,)),
            pltpu.SemaphoreType.DMA((shards,)),
            pltpu.SemaphoreType.DMA((shards,)),
            pltpu.SemaphoreType.DMA((3,)),
            pltpu.SemaphoreType.DMA((3,)),
        ],
        compiler_params=pltpu.CompilerParams(
            collective_id=0, has_side_effects=True, vmem_limit_bytes=LIMIT
        ),
    )(
        frames.reshape(cells, channels),
        w_conv,
        w_lat.T,
        dest.transpose(0, 2, 1),
        pick,
        w_embed,
        gain.reshape(1, depth),
        w_qkv.transpose(1, 0, 2),
    )
    out = pl.pallas_call(
        attend_kernel,
        out_shape=jax.ShapeDtypeStruct((slots, columns), BF16),
        in_specs=[VMEM] * 5,
        out_specs=HBM,
        scratch_shapes=[
            pltpu.VMEM((slots, columns), BF16),
            pltpu.SemaphoreType.DMA((columns // HEAD,)),
        ],
        compiler_params=pltpu.CompilerParams(vmem_limit_bytes=LIMIT // 2),
    )(*handed)
    return out.reshape(1, slots, columns)


def solution(mesh):
    in_specs = (
        P("section", "ctx", None, None),
        P(),
        P(),
        P(None, "ctx", None),
        P(None, "ctx"),
        P(),
        P(),
        P(None, None, "mp"),
    )
    return jax.shard_map(
        functools.partial(on_device, mesh.shape["ctx"], mesh.shape["section"]),
        mesh=mesh,
        in_specs=in_specs,
        out_specs=P("section", "ctx", "mp"),
        check_vma=False,
    )
```

```python
import functools

import jax
import jax.numpy as jnp
from jax import lax
from jax.experimental import pallas as pl
from jax.experimental.pallas import tpu as pltpu
from jax.sharding import PartitionSpec as P

HEAD = 128
GROUP = 4
LANES = 128
META = 16
EPS = 1e-06
MESH = pl.DeviceIdType.MESH
F32 = jnp.float32
BF16 = jnp.bfloat16
HBM = pl.BlockSpec(memory_space=pltpu.HBM)
VMEM = pl.BlockSpec(memory_space=pltpu.VMEM)
LIMIT = 56 * 1024 * 1024


def dot(a, b):
    return jnp.dot(a, b, preferred_element_type=F32)


def dot_nt(a, b):
    return lax.dot_general(a, b, (((1,), (1,)), ((), ())), preferred_element_type=F32)


def iota(shape, dim):
    return lax.broadcasted_iota(jnp.int32, shape, dim)


def encode_kernel(
    shards, frame_count, pieces,
    frames_hbm, conv_hbm, lat_hbm, dest_hbm, pick_hbm, embed_hbm, gain_hbm, qkv_hbm,
    weff_out, rows_out, queries_out, keys_out, bias_out,
    frames, conv, lat_ref, dest_ref, pick_ref, embed, gain_ref, qkv, scaled, wide, packed, inbox, total,
    in_sem, qkv_sem, row_send, row_recv, half_send, half_recv,
):
    section = lax.axis_index("section")
    ctx = lax.axis_index("ctx")
    other = 1 - section
    depth = embed.shape[1]
    latent = embed.shape[0]
    half = qkv.shape[2]
    step = depth // pieces
    row_count = dest_ref.shape[2]
    pack = LANES // latent
    lines = row_count // pack

    cells, channels = frames.shape
    chunks = 2
    chunk = channels // chunks

    barrier = pltpu.get_barrier_semaphore()
    for d in range(shards):
        pl.semaphore_signal(
            barrier, inc=1,
            device_id={"section": other, "ctx": lax.rem(ctx + d, shards)}, device_id_type=MESH,
        )
    loads = [
        pltpu.make_async_copy(source, target, in_sem.at[i])
        for i, (source, target) in enumerate((
            (dest_hbm, dest_ref), (pick_hbm, pick_ref), (lat_hbm, lat_ref), (gain_hbm, gain_ref),
            (embed_hbm, embed), (frames_hbm, frames),
        ) + tuple(
            (conv_hbm.at[:, :, pl.ds(n * chunk, chunk)], conv.at[:, :, pl.ds(n * chunk, chunk)])
            for n in range(chunks)
        ))
    ]
    for load in loads:
        load.start()
    columns = pl.ds(pl.multiple_of(section * half, LANES), half)

    def stream(j, p):
        part = pl.ds(pl.multiple_of(p * step, step), step)
        return pltpu.make_async_copy(
            qkv_hbm.at[j, part, columns], qkv.at[j, part, :], qkv_sem.at[j * pieces + p]
        )

    loads[0].wait()
    loads[1].wait()
    first = section == 0
    dest = jnp.where(first, dest_ref[0], dest_ref[1])
    pick = jnp.where(first, pick_ref[0:1, :], pick_ref[1:2, :])
    tier = (pick >= 4).astype(jnp.int32) + (pick >= 6).astype(jnp.int32)
    label = dest // GROUP + shards // GROUP * tier + 1
    padded = -(-shards // 8) * 8
    onehot = (iota((padded, row_count), 0) == dest).astype(F32)
    earlier = (iota((row_count, row_count), 0) < iota((row_count, row_count), 1)).astype(F32)
    before = dot(onehot.astype(BF16), earlier.astype(BF16))
    within = jnp.sum(before * onehot, axis=0, keepdims=True)
    line = iota((META, row_count), 0)
    meta = jnp.where(line == 0, dest.astype(F32), 0.0)
    meta = jnp.where(line == 1, within, meta)
    meta = jnp.where(line == 2, label.astype(F32), meta)
    packed[lines:, :] = meta.astype(BF16)
    frame = cells // frame_count
    classes = lat_ref.shape[0]
    per = latent // classes
    for load in loads[2:5]:
        load.wait()
    for j in range(1):
        for p in range(pieces):
            stream(j, p).start()

    tile = 512
    for k in range(depth // tile):
        part = slice(k * tile, (k + 1) * tile)
        full = embed[:, part].astype(F32) * gain_ref[:, part]
        top = full.astype(BF16)
        scaled[:latent, part] = top
        scaled[latent:, part] = (full - top.astype(F32)).astype(BF16)
    gram = dot_nt(embed[...], embed[...]) * (1.0 / depth)
    loads[5].wait()
    for j in range(1, 3):
        for p in range(pieces):
            stream(j, p).start()

    x = frames[...]
    back = [x]
    for t in range(1, conv.shape[0]):
        back.append(jnp.concatenate(
            [jnp.zeros((t * frame, channels), BF16), frames[: cells - t * frame, :]], axis=0
        ))
    x = jnp.concatenate(back, axis=1)
    narrow = lat_ref[...]
    spread = jnp.concatenate([narrow] * (LANES // classes), axis=0)
    for n in range(chunks):
        loads[6 + n].wait()
        part = slice(n * chunk, (n + 1) * chunk)
        taps = jnp.concatenate([conv[t, :, part] for t in range(conv.shape[0])], axis=0)
        value = dot(x, taps)
        value = 0.5 * value
        active = (value * jnp.tanh(value) + value).astype(BF16)
        partial = dot_nt(active, spread[:, part])
        if n == 0:
            wide[...] = partial
        else:
            wide[...] += partial
    patches = jnp.zeros((row_count, LANES), F32)
    lane = iota((row_count, LANES), 1)
    for i in range(per):
        cell = wide[pl.ds(i, row_count, stride=per), :].astype(BF16).astype(F32)
        patches = jnp.where(lane // classes == i, cell, patches)
    slim = patches[:, :latent]
    exact = slim.astype(BF16)
    image = jnp.zeros((row_count, latent), F32)
    rest = gram
    for _ in range(3):
        piece = rest.astype(BF16)
        rest = rest - piece.astype(F32)
        image = image + dot(exact, piece)
    square = jnp.sum(slim * image, axis=1, keepdims=True)
    patches = patches * lax.rsqrt(jnp.maximum(square, 0.0) + EPS)
    joined = patches[:lines, :]
    for i in range(1, pack):
        joined = joined + pltpu.roll(patches[i * lines : (i + 1) * lines, :], i * latent, 1)
    packed[:lines, :] = joined.astype(BF16)

    def swap(j):
        return pltpu.make_async_remote_copy(
            src_ref=weff_out.at[section, j], dst_ref=weff_out.at[section, j],
            send_sem=half_send.at[j], recv_sem=half_recv.at[j],
            device_id={"section": other}, device_id_type=MESH,
        )

    def post(t):
        return pltpu.make_async_remote_copy(
            src_ref=packed, dst_ref=inbox.at[ctx], send_sem=row_send.at[t], recv_sem=row_recv.at[ctx],
            device_id={"section": other, "ctx": t}, device_id_type=MESH,
        )

    def arrival(c):
        return pltpu.make_async_remote_copy(
            src_ref=packed, dst_ref=inbox.at[c], send_sem=row_send.at[c], recv_sem=row_recv.at[c],
            device_id={"section": other, "ctx": c}, device_id_type=MESH,
        )

    def contract(j):
        total[...] = jnp.zeros_like(total)

        def piece(p, inner):
            stream(j, p).wait()
            part = pl.ds(pl.multiple_of(p * step, step), step)
            total[...] += dot(scaled[:, part], qkv[j, part, :])
            return inner

        lax.fori_loop(0, pieces, piece, 0)
        full = total[...]
        weff_out[section, j] = (full[:latent] + full[latent:]).astype(BF16)

    early = ctx == 0

    @pl.when(early)
    def _():
        contract(0)

    pl.semaphore_wait(barrier, shards)
    for t in range(shards):
        post(t).start()

    @pl.when(jnp.logical_not(early))
    def _():
        contract(0)

    swap(0).start()

    def later(j, carry):
        contract(j)
        swap(j).start()
        return carry

    lax.fori_loop(1, 3, later, 0)
    sections = weff_out.shape[0]

    def head_norm(x, factor):
        return x * (lax.rsqrt(jnp.mean(x * x, axis=-1, keepdims=True) + EPS) * factor)

    def project(x, j, out, first_row, factor):
        count = x.shape[0]
        for i in range(sections):
            y = dot(x, weff_out[i, j])
            for h in range(half // HEAD):
                z = head_norm(y[:, h * HEAD : (h + 1) * HEAD], factor).astype(BF16)
                out[first_row : first_row + count, i * half + h * HEAD : i * half + (h + 1) * HEAD] = z

    swap(0).wait_recv()
    swap(1).wait_recv()
    capacity = queries_out.shape[0] // shards
    slots = queries_out.shape[0]
    labels, spots = [], []
    for c in range(shards):
        arrival(c).wait_recv()
        both = inbox[c, :lines, :]
        block = jnp.concatenate([both[:, i * latent : (i + 1) * latent] for i in range(pack)], axis=0)
        rows_out[c * row_count : (c + 1) * row_count, :] = block
        project(block, 1, keys_out, c * row_count, 1.0)
        meta = inbox[c, lines:, :].astype(F32)
        labels.append(meta[2:3, :])
        spots.append(jnp.where(meta[0:1, :] == ctx.astype(F32), meta[1:2, :] + (c * capacity), -1.0))
    label = jnp.concatenate(labels, axis=1)
    spot = jnp.concatenate(spots, axis=1).astype(jnp.int32)
    taken = spot == iota((slots, spot.shape[1]), 0)
    picked = dot(taken.astype(F32).astype(BF16), rows_out[...]).astype(BF16)
    own = jnp.sum(jnp.where(taken, label, 0.0), axis=1, keepdims=True)
    bias_out[...] = jnp.where(label == own, 0.0, -1e30)
    project(picked, 0, queries_out, 0, 1.0 / HEAD**0.5)
    for t in range(shards):
        post(t).wait_send()
    for j in range(3):
        swap(j).wait_send()
    swap(2).wait_recv()


def attend_kernel(weff_ref, rows_ref, queries_ref, keys_ref, bias_ref, out_hbm, out_ref, sem):
    sections, _, _, half = weff_ref.shape
    rows = rows_ref[...]
    copies = []
    group = min(2, half // HEAD)
    pair = group * HEAD
    for i in range(sections):
        for g in range(half // pair):
            v = dot(rows, weff_ref[i, 2, :, g * pair : (g + 1) * pair]).astype(BF16)
            for h in range(group):
                where = slice(i * half + g * pair + h * HEAD, i * half + g * pair + (h + 1) * HEAD)
                expo = jnp.exp(dot_nt(queries_ref[:, where], keys_ref[:, where]) + bias_ref[...])
                den = jnp.sum(expo, axis=1, keepdims=True)
                summed = dot(expo.astype(BF16), v[:, h * HEAD : (h + 1) * HEAD])
                out_ref[:, where] = (summed * (1.0 / jnp.where(den > 0.0, den, 1.0))).astype(BF16)
            where = pl.ds(i * half + g * pair, pair)
            copy = pltpu.make_async_copy(out_ref.at[:, where], out_hbm.at[:, where], sem.at[len(copies)])
            copy.start()
            copies.append(copy)
    for copy in copies:
        copy.wait()


def on_device(shards, sections, frames, w_conv, w_lat, dest, pick, w_embed, gain, w_qkv):
    _, frame_count, frame, channels = frames.shape
    latent, depth = w_embed.shape
    cells = frame_count * frame
    row_count = dest.shape[1]
    columns = w_qkv.shape[2]
    half = columns // sections
    pieces = 4
    capacity = max(2, 3 * row_count // (2 * shards))
    slots = shards * capacity
    lines = row_count * latent // LANES
    total_rows = shards * row_count
    handed = pl.pallas_call(
        functools.partial(encode_kernel, shards, frame_count, pieces),
        out_shape=(
            pltpu.VMEM((sections, 3, latent, half), BF16),
            pltpu.VMEM((total_rows, latent), BF16),
            pltpu.VMEM((slots, columns), BF16),
            pltpu.VMEM((total_rows, columns), BF16),
            pltpu.VMEM((slots, total_rows), F32),
        ),
        in_specs=[HBM] * 8,
        out_specs=(VMEM,) * 5,
        scratch_shapes=[
            pltpu.VMEM((cells, channels), BF16),
            pltpu.VMEM(w_conv.shape, BF16),
            pltpu.VMEM((w_lat.shape[1], channels), BF16),
            pltpu.VMEM((sections, 1, row_count), jnp.int32),
            pltpu.VMEM((sections, row_count), jnp.int32),
            pltpu.VMEM((latent, depth), BF16),
            pltpu.VMEM((1, depth), F32),
            pltpu.VMEM((3, depth, half), BF16),
            pltpu.VMEM((2 * latent, depth), BF16),
            pltpu.VMEM((cells, LANES), F32),
            pltpu.VMEM((lines + META, LANES), BF16),
            pltpu.VMEM((shards, lines + META, LANES), BF16),
            pltpu.VMEM((2 * latent, half), F32),
            pltpu.SemaphoreType.DMA((8,)),
            pltpu.SemaphoreType.DMA((3 * pieces,)),
            pltpu.SemaphoreType.DMA((shards,)),
            pltpu.SemaphoreType.DMA((shards,)),
            pltpu.SemaphoreType.DMA((3,)),
            pltpu.SemaphoreType.DMA((3,)),
        ],
        compiler_params=pltpu.CompilerParams(
            collective_id=0, has_side_effects=True, vmem_limit_bytes=LIMIT
        ),
    )(
        frames.reshape(cells, channels),
        w_conv,
        w_lat.T,
        dest.transpose(0, 2, 1),
        pick,
        w_embed,
        gain.reshape(1, depth),
        w_qkv.transpose(1, 0, 2),
    )
    out = pl.pallas_call(
        attend_kernel,
        out_shape=jax.ShapeDtypeStruct((slots, columns), BF16),
        in_specs=[VMEM] * 5,
        out_specs=HBM,
        scratch_shapes=[
            pltpu.VMEM((slots, columns), BF16),
            pltpu.SemaphoreType.DMA((columns // HEAD,)),
        ],
        compiler_params=pltpu.CompilerParams(vmem_limit_bytes=LIMIT // 2),
    )(*handed)
    return out.reshape(1, slots, columns)


def solution(mesh):
    in_specs = (
        P("section", "ctx", None, None),
        P(),
        P(),
        P(None, "ctx", None),
        P(None, "ctx"),
        P(),
        P(),
        P(None, None, "mp"),
    )
    return jax.shard_map(
        functools.partial(on_device, mesh.shape["ctx"], mesh.shape["section"]),
        mesh=mesh,
        in_specs=in_specs,
        out_specs=P("section", "ctx", "mp"),
        check_vma=False,
    )
```

```python
import functools

import jax
import jax.numpy as jnp
from jax import lax
from jax.experimental import pallas as pl
from jax.experimental.pallas import tpu as pltpu
from jax.sharding import PartitionSpec as P

HEAD = 128
GROUP = 4
LANES = 128
META = 16
EPS = 1e-06
MESH = pl.DeviceIdType.MESH
F32 = jnp.float32
BF16 = jnp.bfloat16
HBM = pl.BlockSpec(memory_space=pltpu.HBM)
VMEM = pl.BlockSpec(memory_space=pltpu.VMEM)
LIMIT = 56 * 1024 * 1024


def dot(a, b):
    return jnp.dot(a, b, preferred_element_type=F32)


def dot_nt(a, b):
    return lax.dot_general(a, b, (((1,), (1,)), ((), ())), preferred_element_type=F32)


def iota(shape, dim):
    return lax.broadcasted_iota(jnp.int32, shape, dim)


def encode_kernel(
    shards, frame_count, pieces,
    frames_hbm, conv_hbm, lat_hbm, dest_hbm, pick_hbm, embed_hbm, gain_hbm, qkv_hbm,
    weff_out, rows_out, queries_out, keys_out, bias_out,
    frames, conv, lat_ref, dest_ref, pick_ref, embed, gain_ref, qkv, scaled, wide, packed, inbox, total,
    in_sem, qkv_sem, row_send, row_recv, half_send, half_recv,
):
    section = lax.axis_index("section")
    ctx = lax.axis_index("ctx")
    other = 1 - section
    depth = embed.shape[1]
    latent = embed.shape[0]
    half = qkv.shape[2]
    step = depth // pieces
    row_count = dest_ref.shape[2]
    pack = LANES // latent
    lines = row_count // pack

    cells, channels = frames.shape
    chunks = 2
    chunk = channels // chunks

    barrier = pltpu.get_barrier_semaphore()
    for d in range(shards):
        pl.semaphore_signal(
            barrier, inc=1,
            device_id={"section": other, "ctx": lax.rem(ctx + d, shards)}, device_id_type=MESH,
        )
    loads = [
        pltpu.make_async_copy(source, target, in_sem.at[i])
        for i, (source, target) in enumerate((
            (dest_hbm, dest_ref), (pick_hbm, pick_ref), (lat_hbm, lat_ref), (gain_hbm, gain_ref),
            (embed_hbm, embed), (frames_hbm, frames),
        ) + tuple(
            (conv_hbm.at[:, :, pl.ds(n * chunk, chunk)], conv.at[:, :, pl.ds(n * chunk, chunk)])
            for n in range(chunks)
        ))
    ]
    for load in loads:
        load.start()
    columns = pl.ds(pl.multiple_of(section * half, LANES), half)

    def stream(j, p):
        part = pl.ds(pl.multiple_of(p * step, step), step)
        return pltpu.make_async_copy(
            qkv_hbm.at[j, part, columns], qkv.at[j, part, :], qkv_sem.at[j * pieces + p]
        )

    loads[0].wait()
    loads[1].wait()
    first = section == 0
    dest = jnp.where(first, dest_ref[0], dest_ref[1])
    pick = jnp.where(first, pick_ref[0:1, :], pick_ref[1:2, :])
    tier = (pick >= 4).astype(jnp.int32) + (pick >= 6).astype(jnp.int32)
    label = dest // GROUP + shards // GROUP * tier + 1
    padded = -(-shards // 8) * 8
    onehot = (iota((padded, row_count), 0) == dest).astype(F32)
    earlier = (iota((row_count, row_count), 0) < iota((row_count, row_count), 1)).astype(F32)
    before = dot(onehot.astype(BF16), earlier.astype(BF16))
    within = jnp.sum(before * onehot, axis=0, keepdims=True)
    line = iota((META, row_count), 0)
    meta = jnp.where(line == 0, dest.astype(F32), 0.0)
    meta = jnp.where(line == 1, within, meta)
    meta = jnp.where(line == 2, label.astype(F32), meta)
    packed[lines:, :] = meta.astype(BF16)
    frame = cells // frame_count
    classes = lat_ref.shape[0]
    per = latent // classes
    for load in loads[2:5]:
        load.wait()
    for j in range(1):
        for p in range(pieces):
            stream(j, p).start()

    tile = 512
    gram = dot_nt(embed[...], embed[...]) * (1.0 / depth)
    loads[5].wait()
    for j in range(1, 3):
        for p in range(pieces):
            stream(j, p).start()

    x = frames[...]
    back = [x]
    for t in range(1, conv.shape[0]):
        back.append(jnp.concatenate(
            [jnp.zeros((t * frame, channels), BF16), frames[: cells - t * frame, :]], axis=0
        ))
    x = jnp.concatenate(back, axis=1)
    narrow = lat_ref[...]
    spread = jnp.concatenate([narrow] * (LANES // classes), axis=0)
    for n in range(chunks):
        if n == 0:
            loads[6].wait()
            loads[7].wait()
        part = slice(n * chunk, (n + 1) * chunk)
        taps = jnp.concatenate([conv[t, :, part] for t in range(conv.shape[0])], axis=0)
        value = dot(x, taps)
        value = 0.5 * value
        active = (value * jnp.tanh(value) + value).astype(BF16)
        partial = dot_nt(active, spread[:, part])
        if n == 0:
            wide[...] = partial
        else:
            wide[...] += partial
    patches = jnp.zeros((row_count, LANES), F32)
    lane = iota((row_count, LANES), 1)
    for i in range(per):
        cell = wide[pl.ds(i, row_count, stride=per), :].astype(BF16).astype(F32)
        patches = jnp.where(lane // classes == i, cell, patches)
    slim = patches[:, :latent]
    exact = slim.astype(BF16)
    image = jnp.zeros((row_count, latent), F32)
    rest = gram
    for _ in range(3):
        piece = rest.astype(BF16)
        rest = rest - piece.astype(F32)
        image = image + dot(exact, piece)
    square = jnp.sum(slim * image, axis=1, keepdims=True)
    patches = patches * lax.rsqrt(jnp.maximum(square, 0.0) + EPS)
    joined = patches[:lines, :]
    for i in range(1, pack):
        joined = joined + pltpu.roll(patches[i * lines : (i + 1) * lines, :], i * latent, 1)
    packed[:lines, :] = joined.astype(BF16)

    def swap(j):
        return pltpu.make_async_remote_copy(
            src_ref=weff_out.at[section, j], dst_ref=weff_out.at[section, j],
            send_sem=half_send.at[j], recv_sem=half_recv.at[j],
            device_id={"section": other}, device_id_type=MESH,
        )

    def post(t):
        return pltpu.make_async_remote_copy(
            src_ref=packed, dst_ref=inbox.at[ctx], send_sem=row_send.at[t], recv_sem=row_recv.at[ctx],
            device_id={"section": other, "ctx": t}, device_id_type=MESH,
        )

    def arrival(c):
        return pltpu.make_async_remote_copy(
            src_ref=packed, dst_ref=inbox.at[c], send_sem=row_send.at[c], recv_sem=row_recv.at[c],
            device_id={"section": other, "ctx": c}, device_id_type=MESH,
        )

    def contract(j):
        total[...] = jnp.zeros_like(total)

        def piece(p, inner):
            stream(j, p).wait()
            part = pl.ds(pl.multiple_of(p * step, step), step)
            total[...] += dot(scaled[:, part], qkv[j, part, :])
            return inner

        lax.fori_loop(0, pieces, piece, 0)
        weff_out[section, j] = total[...].astype(BF16)

    early = ctx == 0

    def scale_embed():
        for k in range(depth // tile):
            part = slice(k * tile, (k + 1) * tile)
            scaled[:, part] = (embed[:, part].astype(F32) * gain_ref[:, part]).astype(BF16)

    @pl.when(early)
    def _():
        scale_embed()
        contract(0)

    pl.semaphore_wait(barrier, shards)
    for t in range(shards):
        post(t).start()

    @pl.when(jnp.logical_not(early))
    def _():
        scale_embed()
        contract(0)

    swap(0).start()

    def later(j, carry):
        contract(j)
        swap(j).start()
        return carry

    lax.fori_loop(1, 3, later, 0)
    sections = weff_out.shape[0]

    pair = min(2 * HEAD, half)
    same_head = iota((pair, pair), 0) // HEAD == iota((pair, pair), 1) // HEAD
    average = jnp.where(same_head, 1.0 / HEAD, 0.0).astype(BF16)

    def project(x, j, out, first_row, factor):
        count = x.shape[0]
        for i in range(sections):
            for g in range(half // pair):
                y = dot(x, weff_out[i, j, :, g * pair : (g + 1) * pair])
                mean = dot((y * y).astype(BF16), average)
                z = (y * (lax.rsqrt(mean + EPS) * factor)).astype(BF16)
                out[first_row : first_row + count, i * half + g * pair : i * half + (g + 1) * pair] = z

    swap(0).wait_recv()
    swap(1).wait_recv()
    capacity = queries_out.shape[0] // shards
    slots = queries_out.shape[0]
    labels, spots = [], []
    for c in range(shards):
        arrival(c).wait_recv()
        both = inbox[c, :lines, :]
        block = jnp.concatenate([both[:, i * latent : (i + 1) * latent] for i in range(pack)], axis=0)
        rows_out[c * row_count : (c + 1) * row_count, :] = block
        project(block, 1, keys_out, c * row_count, 1.0)
        meta = inbox[c, lines:, :].astype(F32)
        labels.append(meta[2:3, :])
        spots.append(jnp.where(meta[0:1, :] == ctx.astype(F32), meta[1:2, :] + (c * capacity), -1.0))
    label = jnp.concatenate(labels, axis=1)
    spot = jnp.concatenate(spots, axis=1).astype(jnp.int32)
    taken = spot == iota((slots, spot.shape[1]), 0)
    picked = dot(taken.astype(F32).astype(BF16), rows_out[...]).astype(BF16)
    own = jnp.sum(jnp.where(taken, label, 0.0), axis=1, keepdims=True)
    bias_out[...] = jnp.where(label == own, 0.0, -1e30)
    project(picked, 0, queries_out, 0, 1.0 / HEAD**0.5)
    for t in range(shards):
        post(t).wait_send()
    for j in range(3):
        swap(j).wait_send()
    swap(2).wait_recv()


def attend_kernel(weff_ref, rows_ref, queries_ref, keys_ref, bias_ref, out_hbm, out_ref, sem):
    sections, _, _, half = weff_ref.shape
    rows = rows_ref[...]
    copies = []
    group = min(2, half // HEAD)
    pair = group * HEAD
    for i in range(sections):
        for g in range(half // pair):
            v = dot(rows, weff_ref[i, 2, :, g * pair : (g + 1) * pair]).astype(BF16)
            for h in range(group):
                where = slice(i * half + g * pair + h * HEAD, i * half + g * pair + (h + 1) * HEAD)
                expo = jnp.exp(dot_nt(queries_ref[:, where], keys_ref[:, where]) + bias_ref[...])
                den = jnp.sum(expo, axis=1, keepdims=True)
                summed = dot(expo.astype(BF16), v[:, h * HEAD : (h + 1) * HEAD])
                out_ref[:, where] = (summed * (1.0 / jnp.where(den > 0.0, den, 1.0))).astype(BF16)
            where = pl.ds(i * half + g * pair, pair)
            copy = pltpu.make_async_copy(out_ref.at[:, where], out_hbm.at[:, where], sem.at[len(copies)])
            copy.start()
            copies.append(copy)
    for copy in copies:
        copy.wait()


def on_device(shards, sections, frames, w_conv, w_lat, dest, pick, w_embed, gain, w_qkv):
    _, frame_count, frame, channels = frames.shape
    latent, depth = w_embed.shape
    cells = frame_count * frame
    row_count = dest.shape[1]
    columns = w_qkv.shape[2]
    half = columns // sections
    pieces = 2
    capacity = max(2, 3 * row_count // (2 * shards))
    slots = shards * capacity
    lines = row_count * latent // LANES
    total_rows = shards * row_count
    handed = pl.pallas_call(
        functools.partial(encode_kernel, shards, frame_count, pieces),
        out_shape=(
            pltpu.VMEM((sections, 3, latent, half), BF16),
            pltpu.VMEM((total_rows, latent), BF16),
            pltpu.VMEM((slots, columns), BF16),
            pltpu.VMEM((total_rows, columns), BF16),
            pltpu.VMEM((slots, total_rows), F32),
        ),
        in_specs=[HBM] * 8,
        out_specs=(VMEM,) * 5,
        scratch_shapes=[
            pltpu.VMEM((cells, channels), BF16),
            pltpu.VMEM(w_conv.shape, BF16),
            pltpu.VMEM((w_lat.shape[1], channels), BF16),
            pltpu.VMEM((sections, 1, row_count), jnp.int32),
            pltpu.VMEM((sections, row_count), jnp.int32),
            pltpu.VMEM((latent, depth), BF16),
            pltpu.VMEM((1, depth), F32),
            pltpu.VMEM((3, depth, half), BF16),
            pltpu.VMEM((latent, depth), BF16),
            pltpu.VMEM((cells, LANES), F32),
            pltpu.VMEM((lines + META, LANES), BF16),
            pltpu.VMEM((shards, lines + META, LANES), BF16),
            pltpu.VMEM((latent, half), F32),
            pltpu.SemaphoreType.DMA((8,)),
            pltpu.SemaphoreType.DMA((3 * pieces,)),
            pltpu.SemaphoreType.DMA((shards,)),
            pltpu.SemaphoreType.DMA((shards,)),
            pltpu.SemaphoreType.DMA((3,)),
            pltpu.SemaphoreType.DMA((3,)),
        ],
        compiler_params=pltpu.CompilerParams(
            collective_id=0, has_side_effects=True, vmem_limit_bytes=LIMIT
        ),
    )(
        frames.reshape(cells, channels),
        w_conv,
        w_lat.T,
        dest.transpose(0, 2, 1),
        pick,
        w_embed,
        gain.reshape(1, depth),
        w_qkv.transpose(1, 0, 2),
    )
    out = pl.pallas_call(
        attend_kernel,
        out_shape=jax.ShapeDtypeStruct((slots, columns), BF16),
        in_specs=[VMEM] * 5,
        out_specs=HBM,
        scratch_shapes=[
            pltpu.VMEM((slots, columns), BF16),
            pltpu.SemaphoreType.DMA((columns // HEAD,)),
        ],
        compiler_params=pltpu.CompilerParams(vmem_limit_bytes=LIMIT // 2),
    )(*handed)
    return out.reshape(1, slots, columns)


def solution(mesh):
    in_specs = (
        P("section", "ctx", None, None),
        P(),
        P(),
        P(None, "ctx", None),
        P(None, "ctx"),
        P(),
        P(),
        P(None, None, "mp"),
    )
    return jax.shard_map(
        functools.partial(on_device, mesh.shape["ctx"], mesh.shape["section"]),
        mesh=mesh,
        in_specs=in_specs,
        out_specs=P("section", "ctx", "mp"),
        check_vma=False,
    )
```

```python
import functools

import jax
import jax.numpy as jnp
from jax import lax
from jax.experimental import pallas as pl
from jax.experimental.pallas import tpu as pltpu
from jax.sharding import PartitionSpec as P

HEAD = 128
GROUP = 4
LANES = 128
META = 16
EPS = 1e-06
MESH = pl.DeviceIdType.MESH
F32 = jnp.float32
BF16 = jnp.bfloat16
HBM = pl.BlockSpec(memory_space=pltpu.HBM)
VMEM = pl.BlockSpec(memory_space=pltpu.VMEM)
LIMIT = 56 * 1024 * 1024


def dot(a, b):
    return jnp.dot(a, b, preferred_element_type=F32)


def dot_nt(a, b):
    return lax.dot_general(a, b, (((1,), (1,)), ((), ())), preferred_element_type=F32)


def iota(shape, dim):
    return lax.broadcasted_iota(jnp.int32, shape, dim)


def encode_kernel(
    shards, frame_count, pieces,
    frames_hbm, conv_hbm, lat_hbm, dest_hbm, pick_hbm, embed_hbm, gain_hbm, qkv_hbm,
    weff_out, rows_out, queries_out, keys_out, bias_out,
    frames, conv, lat_ref, dest_ref, pick_ref, embed, gain_ref, qkv, scaled, wide, packed, inbox, total,
    in_sem, qkv_sem, row_send, row_recv, half_send, half_recv,
):
    section = lax.axis_index("section")
    ctx = lax.axis_index("ctx")
    other = 1 - section
    depth = embed.shape[1]
    latent = embed.shape[0]
    half = qkv.shape[2]
    step = depth // pieces
    row_count = dest_ref.shape[2]
    pack = LANES // latent
    lines = row_count // pack

    cells, channels = frames.shape
    chunks = 2
    chunk = channels // chunks

    barrier = pltpu.get_barrier_semaphore()
    for d in range(shards):
        pl.semaphore_signal(
            barrier, inc=1,
            device_id={"section": other, "ctx": lax.rem(ctx + d, shards)}, device_id_type=MESH,
        )
    loads = [
        pltpu.make_async_copy(source, target, in_sem.at[i])
        for i, (source, target) in enumerate((
            (dest_hbm, dest_ref), (pick_hbm, pick_ref), (lat_hbm, lat_ref), (gain_hbm, gain_ref),
            (embed_hbm, embed), (frames_hbm, frames),
        ) + tuple(
            (conv_hbm.at[:, :, pl.ds(n * chunk, chunk)], conv.at[:, :, pl.ds(n * chunk, chunk)])
            for n in range(chunks)
        ))
    ]
    for load in loads:
        load.start()
    columns = pl.ds(pl.multiple_of(section * half, LANES), half)

    def stream(j, p):
        part = pl.ds(pl.multiple_of(p * step, step), step)
        return pltpu.make_async_copy(
            qkv_hbm.at[j, part, columns], qkv.at[j, part, :], qkv_sem.at[j * pieces + p]
        )

    loads[0].wait()
    loads[1].wait()
    first = section == 0
    dest = jnp.where(first, dest_ref[0], dest_ref[1])
    pick = jnp.where(first, pick_ref[0:1, :], pick_ref[1:2, :])
    tier = (pick >= 4).astype(jnp.int32) + (pick >= 6).astype(jnp.int32)
    label = dest // GROUP + shards // GROUP * tier + 1
    padded = -(-shards // 8) * 8
    onehot = (iota((padded, row_count), 0) == dest).astype(F32)
    earlier = (iota((row_count, row_count), 0) < iota((row_count, row_count), 1)).astype(F32)
    before = dot(onehot.astype(BF16), earlier.astype(BF16))
    within = jnp.sum(before * onehot, axis=0, keepdims=True)
    line = iota((META, row_count), 0)
    meta = jnp.where(line == 0, dest.astype(F32), 0.0)
    meta = jnp.where(line == 1, within, meta)
    meta = jnp.where(line == 2, label.astype(F32), meta)
    packed[lines:, :] = meta.astype(BF16)
    frame = cells // frame_count
    classes = lat_ref.shape[0]
    per = latent // classes
    for load in loads[2:5]:
        load.wait()
    for j in range(1):
        for p in range(pieces):
            stream(j, p).start()

    tile = 512
    gram = dot_nt(embed[...], embed[...]) * (1.0 / depth)
    loads[5].wait()
    for j in range(1, 3):
        for p in range(pieces):
            stream(j, p).start()

    x = frames[...]
    back = [x]
    for t in range(1, conv.shape[0]):
        back.append(jnp.concatenate(
            [jnp.zeros((t * frame, channels), BF16), frames[: cells - t * frame, :]], axis=0
        ))
    x = jnp.concatenate(back, axis=1)
    narrow = lat_ref[...]
    spread = jnp.concatenate([narrow] * (LANES // classes), axis=0)
    for n in range(chunks):
        if n == 0:
            loads[6].wait()
            loads[7].wait()
        part = slice(n * chunk, (n + 1) * chunk)
        taps = jnp.concatenate([conv[t, :, part] for t in range(conv.shape[0])], axis=0)
        value = dot(x, taps)
        value = 0.5 * value
        active = (value * jnp.tanh(value) + value).astype(BF16)
        partial = dot_nt(active, spread[:, part])
        if n == 0:
            wide[...] = partial
        else:
            wide[...] += partial
    patches = jnp.zeros((row_count, LANES), F32)
    lane = iota((row_count, LANES), 1)
    for i in range(per):
        cell = wide[pl.ds(i, row_count, stride=per), :].astype(BF16).astype(F32)
        patches = jnp.where(lane // classes == i, cell, patches)
    slim = patches[:, :latent]
    exact = slim.astype(BF16)
    image = jnp.zeros((row_count, latent), F32)
    rest = gram
    for _ in range(3):
        piece = rest.astype(BF16)
        rest = rest - piece.astype(F32)
        image = image + dot(exact, piece)
    square = jnp.sum(slim * image, axis=1, keepdims=True)
    patches = patches * lax.rsqrt(jnp.maximum(square, 0.0) + EPS)
    joined = patches[:lines, :]
    for i in range(1, pack):
        joined = joined + pltpu.roll(patches[i * lines : (i + 1) * lines, :], i * latent, 1)
    packed[:lines, :] = joined.astype(BF16)

    def swap(j):
        return pltpu.make_async_remote_copy(
            src_ref=weff_out.at[section, j], dst_ref=weff_out.at[section, j],
            send_sem=half_send.at[j], recv_sem=half_recv.at[j],
            device_id={"section": other}, device_id_type=MESH,
        )

    def post(t):
        return pltpu.make_async_remote_copy(
            src_ref=packed, dst_ref=inbox.at[ctx], send_sem=row_send.at[t], recv_sem=row_recv.at[ctx],
            device_id={"section": other, "ctx": t}, device_id_type=MESH,
        )

    def arrival(c):
        return pltpu.make_async_remote_copy(
            src_ref=packed, dst_ref=inbox.at[c], send_sem=row_send.at[c], recv_sem=row_recv.at[c],
            device_id={"section": other, "ctx": c}, device_id_type=MESH,
        )

    def contract(j):
        total[...] = jnp.zeros_like(total)

        def piece(p, inner):
            stream(j, p).wait()
            part = pl.ds(pl.multiple_of(p * step, step), step)
            total[...] += dot(scaled[:, part], qkv[j, part, :])
            return inner

        lax.fori_loop(0, pieces, piece, 0)
        weff_out[section, j] = total[...].astype(BF16)

    early = ctx == 0

    def scale_embed():
        for k in range(depth // tile):
            part = slice(k * tile, (k + 1) * tile)
            scaled[:, part] = (embed[:, part].astype(F32) * gain_ref[:, part]).astype(BF16)

    @pl.when(early)
    def _():
        scale_embed()
        contract(0)

    pl.semaphore_wait(barrier, shards)
    for t in range(shards):
        post(t).start()

    @pl.when(jnp.logical_not(early))
    def _():
        scale_embed()
        contract(0)

    swap(0).start()

    def later(j, carry):
        contract(j)
        swap(j).start()
        return carry

    lax.fori_loop(1, 3, later, 0)
    sections = weff_out.shape[0]

    pair = min(2 * HEAD, half)
    same_head = iota((pair, pair), 0) // HEAD == iota((pair, pair), 1) // HEAD
    average = jnp.where(same_head, 1.0 / HEAD, 0.0).astype(BF16)

    def project(x, j, out, first_row, factor):
        count = x.shape[0]
        for i in range(sections):
            for g in range(half // pair):
                y = dot(x, weff_out[i, j, :, g * pair : (g + 1) * pair])
                mean = dot((y * y).astype(BF16), average)
                z = (y * (lax.rsqrt(mean + EPS) * factor)).astype(BF16)
                out[first_row : first_row + count, i * half + g * pair : i * half + (g + 1) * pair] = z

    swap(0).wait_recv()
    swap(1).wait_recv()
    capacity = queries_out.shape[0] // shards
    slots = queries_out.shape[0]
    labels, spots = [], []
    groups = [range(c, min(c + 3, shards)) for c in range(0, shards, 3)]
    for group in groups:
        blocks = []
        for c in group:
            arrival(c).wait_recv()
            both = inbox[c, :lines, :]
            blocks += [both[:, i * latent : (i + 1) * latent] for i in range(pack)]
            meta = inbox[c, lines:, :].astype(F32)
            labels.append(meta[2:3, :])
            spots.append(jnp.where(meta[0:1, :] == ctx.astype(F32), meta[1:2, :] + (c * capacity), -1.0))
        block = jnp.concatenate(blocks, axis=0)
        start = group[0] * row_count
        rows_out[start : start + block.shape[0], :] = block
        project(block, 1, keys_out, start, 1.0)
    label = jnp.concatenate(labels, axis=1)
    spot = jnp.concatenate(spots, axis=1).astype(jnp.int32)
    taken = spot == iota((slots, spot.shape[1]), 0)
    picked = dot(taken.astype(F32).astype(BF16), rows_out[...]).astype(BF16)
    own = jnp.sum(jnp.where(taken, label, 0.0), axis=1, keepdims=True)
    bias_out[...] = jnp.where(label == own, 0.0, -1e30)
    project(picked, 0, queries_out, 0, 1.0 / HEAD**0.5)
    for t in range(shards):
        post(t).wait_send()
    for j in range(3):
        swap(j).wait_send()
    swap(2).wait_recv()


def attend_kernel(weff_ref, rows_ref, queries_ref, keys_ref, bias_ref, out_hbm, out_ref, sem):
    sections, _, _, half = weff_ref.shape
    rows = rows_ref[...]
    copies = []
    group = min(2, half // HEAD)
    pair = group * HEAD
    for i in range(sections):
        for g in range(half // pair):
            v = dot(rows, weff_ref[i, 2, :, g * pair : (g + 1) * pair]).astype(BF16)
            for h in range(group):
                where = slice(i * half + g * pair + h * HEAD, i * half + g * pair + (h + 1) * HEAD)
                expo = jnp.exp(dot_nt(queries_ref[:, where], keys_ref[:, where]) + bias_ref[...])
                den = jnp.sum(expo, axis=1, keepdims=True)
                summed = dot(expo.astype(BF16), v[:, h * HEAD : (h + 1) * HEAD])
                out_ref[:, where] = (summed * (1.0 / jnp.where(den > 0.0, den, 1.0))).astype(BF16)
            where = pl.ds(i * half + g * pair, pair)
            copy = pltpu.make_async_copy(out_ref.at[:, where], out_hbm.at[:, where], sem.at[len(copies)])
            copy.start()
            copies.append(copy)
    for copy in copies:
        copy.wait()


def on_device(shards, sections, frames, w_conv, w_lat, dest, pick, w_embed, gain, w_qkv):
    _, frame_count, frame, channels = frames.shape
    latent, depth = w_embed.shape
    cells = frame_count * frame
    row_count = dest.shape[1]
    columns = w_qkv.shape[2]
    half = columns // sections
    pieces = 2
    capacity = max(2, 3 * row_count // (2 * shards))
    slots = shards * capacity
    lines = row_count * latent // LANES
    total_rows = shards * row_count
    handed = pl.pallas_call(
        functools.partial(encode_kernel, shards, frame_count, pieces),
        out_shape=(
            pltpu.VMEM((sections, 3, latent, half), BF16),
            pltpu.VMEM((total_rows, latent), BF16),
            pltpu.VMEM((slots, columns), BF16),
            pltpu.VMEM((total_rows, columns), BF16),
            pltpu.VMEM((slots, total_rows), F32),
        ),
        in_specs=[HBM] * 8,
        out_specs=(VMEM,) * 5,
        scratch_shapes=[
            pltpu.VMEM((cells, channels), BF16),
            pltpu.VMEM(w_conv.shape, BF16),
            pltpu.VMEM((w_lat.shape[1], channels), BF16),
            pltpu.VMEM((sections, 1, row_count), jnp.int32),
            pltpu.VMEM((sections, row_count), jnp.int32),
            pltpu.VMEM((latent, depth), BF16),
            pltpu.VMEM((1, depth), F32),
            pltpu.VMEM((3, depth, half), BF16),
            pltpu.VMEM((latent, depth), BF16),
            pltpu.VMEM((cells, LANES), F32),
            pltpu.VMEM((lines + META, LANES), BF16),
            pltpu.VMEM((shards, lines + META, LANES), BF16),
            pltpu.VMEM((latent, half), F32),
            pltpu.SemaphoreType.DMA((8,)),
            pltpu.SemaphoreType.DMA((3 * pieces,)),
            pltpu.SemaphoreType.DMA((shards,)),
            pltpu.SemaphoreType.DMA((shards,)),
            pltpu.SemaphoreType.DMA((3,)),
            pltpu.SemaphoreType.DMA((3,)),
        ],
        compiler_params=pltpu.CompilerParams(
            collective_id=0, has_side_effects=True, vmem_limit_bytes=LIMIT
        ),
    )(
        frames.reshape(cells, channels),
        w_conv,
        w_lat.T,
        dest.transpose(0, 2, 1),
        pick,
        w_embed,
        gain.reshape(1, depth),
        w_qkv.transpose(1, 0, 2),
    )
    out = pl.pallas_call(
        attend_kernel,
        out_shape=jax.ShapeDtypeStruct((slots, columns), BF16),
        in_specs=[VMEM] * 5,
        out_specs=HBM,
        scratch_shapes=[
            pltpu.VMEM((slots, columns), BF16),
            pltpu.SemaphoreType.DMA((columns // HEAD,)),
        ],
        compiler_params=pltpu.CompilerParams(vmem_limit_bytes=LIMIT // 2),
    )(*handed)
    return out.reshape(1, slots, columns)


def solution(mesh):
    in_specs = (
        P("section", "ctx", None, None),
        P(),
        P(),
        P(None, "ctx", None),
        P(None, "ctx"),
        P(),
        P(),
        P(None, None, "mp"),
    )
    return jax.shard_map(
        functools.partial(on_device, mesh.shape["ctx"], mesh.shape["section"]),
        mesh=mesh,
        in_specs=in_specs,
        out_specs=P("section", "ctx", "mp"),
        check_vma=False,
    )
```
